32 devices in a mesh: hist: 4 (over y, x), row: 4 (over z), cur: 2 (over core).
Axes of the slice: x: 2, y: 2, z: 4, core: 2. Of those that a mesh axis runs over, the one named last changes fastest.
Arguments:
- incident: bfloat16 [4, 32, 256, 64], P(None, ('hist', 'row', 'cur')), may hold values from -6 to 6
- past: bfloat16 [32, 8, 256, 64], P(('hist', 'row', 'cur')), may hold values from -6 to 6
- hist_tiles: bfloat16 [32, 64, 256, 256], P(('hist', 'row', 'cur')), may hold values from -0.046875 to 0.046875
- tile_rows: int32 [32, 64], P(('hist', 'row', 'cur')), may hold values from 0 to 3
- tile_cols: int32 [32, 64], P(('hist', 'row', 'cur')), may hold values from 0 to 7
- tile_lags: int32 [32, 64], P(('hist', 'row', 'cur')), may hold values from 4 to 8
- tile_scales: float32 [32, 64], P(('hist', 'row', 'cur')), may hold values from 0.5 to 2
- near_tiles: bfloat16 [32, 3, 5, 256, 256], P(('hist', 'row', 'cur')), may hold values from -0.09375 to 0.09375
- inverses: bfloat16 [32, 256, 256], P(('hist', 'row', 'cur')), may hold values from -0.21875 to 0.21875
Outputs:
- densities: bfloat16 [4, 32, 256, 64], P(None, ('hist', 'row', 'cur'))
The draws below stay inside these ranges and needn't reach their ends.
All inputs are finite; a program needn't handle non-finite values.
Results may differ from the reference program's by a relative error of at most 0.02.
Values may be sent and summed in bfloat16 or wider, within the bound.
No kernel may reach another device: no remote copies, remote signals or barrier semaphores. Data moves between devices by JAX's collectives and lax.ppermute only.
A program may use at most 128 MiB of HBM per device.

```python
import math
import jax
import jax.numpy as jnp
from jax import lax

BLOCK = 256
ILLUM = 64
STEPS = 4
LAGS = 8
TILES_DEV = 64
PATCHES = 32
GROUPS = 4
LOCAL = 8
N_ROW = 4
N_CUR = 2


def plant(entries, rng, least, high):
    longest = entries.shape.index(max(entries.shape))
    spots = []
    for shift in (0, 1):
        where = [jax.random.randint(jax.random.fold_in(rng, axis), (), 0, length) for axis, length in enumerate(entries.shape)]
        where[longest] = (where[longest] + shift) % entries.shape[longest]
        spots.append(tuple(where))
    return entries.at[spots[0]].set(least).at[spots[1]].set(high)


def shard_levels(rng, dims, shards, smallest, top_value):
    def one(axis_at, parts):
        heights = jax.random.uniform(jax.random.fold_in(jax.random.fold_in(rng, 6), axis_at), (parts,), jnp.float32, smallest / len(shards), top_value / len(shards))
        return jnp.repeat(jnp.exp(heights), dims[axis_at] // parts).reshape((-1,) + (1,) * (len(dims) - axis_at - 1))

    loudness = one(*shards[0])
    for cut in shards[1:]:
        loudness = loudness * one(*cut)
    return loudness


def scatter_about(key, dims, scale, reach, shards=(), held_as=jnp.bfloat16):
    drawn = jax.random.normal(key, dims, jnp.float32) * scale
    if len(shards) > 0:
        drawn = shard_levels(key, dims, shards, -0.22, 0.18) * drawn
    return jnp.clip(drawn, min=-reach, max=reach).astype(held_as)


def setup_inputs(seed: int = 0) -> dict:
    keys = jax.random.split(jax.random.key(seed), 10)
    incident = scatter_about(keys[0], (STEPS, PATCHES, BLOCK, ILLUM), 1.0, 6.0, ((1, 32),))
    past = scatter_about(keys[1], (PATCHES, LAGS, BLOCK, ILLUM), 1.0, 6.0, ((0, 32),))
    hist_tiles = scatter_about(keys[2], (PATCHES, TILES_DEV, BLOCK, BLOCK), (TILES_DEV * BLOCK) ** -0.5, 0.046875, ((0, 32),))
    tile_rows = plant(jax.random.randint(keys[3], (PATCHES, TILES_DEV), 0, GROUPS), jax.random.fold_in(keys[3], 1), 0, GROUPS - 1).astype(jnp.int32)
    tile_cols = plant(jax.random.randint(keys[4], (PATCHES, TILES_DEV), 0, LOCAL), jax.random.fold_in(keys[4], 1), 0, LOCAL - 1).astype(jnp.int32)
    tile_lags = plant(jax.random.randint(keys[5], (PATCHES, TILES_DEV), 4, 9), jax.random.fold_in(keys[5], 1), 4, 8).astype(jnp.int32)
    tile_scales = jnp.clip(jnp.exp(math.log(2.0) - 1.3862944 * jax.random.uniform(keys[6], (PATCHES, TILES_DEV), jnp.float32) ** shard_levels(keys[6], (PATCHES, TILES_DEV), ((0, 32),), -0.2, 0.2)), 0.5, 2.0)
    near_tiles = scatter_about(keys[7], (PATCHES, 3, 5, BLOCK, BLOCK), (15 * BLOCK) ** -0.5, 0.09375, ((0, 32),))
    inverses = scatter_about(keys[8], (PATCHES, BLOCK, BLOCK), (3 * BLOCK) ** -0.5, 0.21875, ((0, 32),))
    return dict(incident=incident, past=past, hist_tiles=hist_tiles, tile_rows=tile_rows, tile_cols=tile_cols, tile_lags=tile_lags, tile_scales=tile_scales, near_tiles=near_tiles, inverses=inverses)


def reference(incident, past, hist_tiles, tile_rows, tile_cols, tile_lags, tile_scales, near_tiles, inverses):
    local_count = N_ROW * N_CUR
    step_ids = jnp.arange(STEPS, dtype=jnp.int32)

    def per_holder(total, holder):
        group = holder // local_count
        slot = holder % local_count
        source = group * local_count + tile_cols[holder]
        when = step_ids[:, None] - tile_lags[holder][None, :] + LAGS
        picked = past[source[None, :], when]
        terms = jnp.einsum('kij,skjr->skir', hist_tiles[holder].astype(jnp.float32), picked.astype(jnp.float32))
        terms = terms * tile_scales[holder][None, :, None, None]
        target = tile_rows[holder] * local_count + slot
        return total.at[:, target].add(terms), None

    start = jnp.zeros((STEPS, PATCHES, BLOCK, ILLUM), jnp.float32)
    history, _ = lax.scan(per_holder, start, jnp.arange(PATCHES, dtype=jnp.int32))

    made = []
    for step in range(STEPS):
        near = jnp.zeros((PATCHES, BLOCK, ILLUM), jnp.float32)
        for lag in range(1, 4):
            when = step - lag
            earlier = past[:, when + LAGS] if when < 0 else made[when]
            padded = jnp.pad(earlier, ((2, 2), (0, 0), (0, 0)))
            for offset in range(-2, 3):
                beside = padded[2 + offset:2 + offset + PATCHES]
                near = near + jnp.einsum('pij,pjr->pir', near_tiles[:, lag - 1, offset + 2].astype(jnp.float32), beside.astype(jnp.float32))
        rhs = (incident[step].astype(jnp.float32) - history[step] - near).astype(jnp.bfloat16)
        fresh = jnp.einsum('pij,pjr->pir', inverses.astype(jnp.float32), rhs.astype(jnp.float32)).astype(jnp.bfloat16)
        made.append(fresh)
    return jnp.stack(made)
```

```python
import functools

import jax
import jax.numpy as jnp
from jax import lax
from jax.experimental import pallas as pl
from jax.experimental.pallas import tpu as pltpu
from jax.sharding import PartitionSpec as P

BATCH = 8


def partner(me, distance, count):
    if count & (count - 1) == 0:
        return me ^ distance
    return (me + distance) % count


def rotated(block, axis, distance):
    count = lax.axis_size(axis)
    return lax.ppermute(block, axis, [(i, (i + distance) % count) for i in range(count)])


def shifted(block, axis, distance):
    count = lax.axis_size(axis)
    return lax.ppermute(block, axis, [(i, i + distance) for i in range(count) if 0 <= i + distance < count])


def swapped(block):
    return lax.ppermute(block, "cur", [(0, 1), (1, 0)])


def in_order(mine, theirs):
    lower = lax.axis_index("cur") == 0
    return jnp.stack([jnp.where(lower, mine, theirs), jnp.where(lower, theirs, mine)])


def halved(block):
    half = block.shape[-2] // 2
    core = lax.axis_index("cur")
    axis = block.ndim - 2
    mine = lax.dynamic_slice_in_dim(block, core * half, half, axis)
    others = lax.dynamic_slice_in_dim(block, (1 - core) * half, half, axis)
    return in_order(mine, swapped(others))


def history_kernel(first, count, kept, n_hist, n_row, n_chunks, *refs):
    pos, rows, cols, lags, scales = refs[:5]
    n_slots = 2 * n_row
    sources = refs[5 : 5 + n_slots * n_chunks]
    tiles = refs[5 + n_slots * n_chunks]
    outs = refs[6 + n_slots * n_chunks : 6 + n_slots * n_chunks + n_hist]
    held, weights, total, held_sem, weight_sem = refs[6 + n_slots * n_chunks + n_hist :]
    tile_count = tiles.shape[0]
    batches = tile_count // BATCH
    illum = outs[0].shape[0] // count

    copies = []
    for slot in range(n_slots):
        start = 0
        for chunk in range(n_chunks):
            source = sources[slot * n_chunks + chunk]
            size = source.shape[0]
            copies.append(
                pltpu.make_async_copy(source, held.at[slot, pl.ds(start, size)], held_sem.at[slot, chunk])
            )
            start += size
    for copy in copies:
        copy.start()

    def load(batch):
        at = pl.ds(batch * BATCH, BATCH)
        return pltpu.make_async_copy(tiles.at[at], weights.at[at], weight_sem.at[batch])

    for batch in range(batches):
        load(batch).start()
    total[...] = jnp.zeros_like(total)
    for copy in copies:
        copy.wait()

    def body(batch, carry):
        load(batch).wait()
        for inner in range(BATCH):
            tile = batch * BATCH + inner
            target = partner_index(rows[tile], pos[0], n_hist)
            column = cols[tile]
            away = lax.rem(pos[1] - lax.div(column, 2) + n_row, n_row)
            slot = jnp.where(lax.rem(column, 2) == pos[2], 0, n_row) + away
            start = pl.multiple_of((first - lags[tile] + kept) * illum, illum)
            x = held[slot, pl.ds(start, count * illum), :]
            y = lax.dot_general(
                x, weights[tile], (((1,), (1,)), ((), ())), preferred_element_type=jnp.float32
            )
            total[target] += y * scales[tile]
        return carry

    lax.fori_loop(0, batches, body, 0)
    for distance in range(n_hist):
        outs[distance][...] = total[distance].astype(outs[distance].dtype)


def partner_index(row, me, count):
    if count & (count - 1) == 0:
        return lax.bitwise_xor(row, me)
    return lax.rem(row - me + count, count)


def history_parts(sources, tiles, rows, cols, lags, scales, pos, first, count, kept, illum, n_hist, n_row):
    n_chunks = len(sources[0])
    size = tiles.shape[-1]
    held_rows = sum(chunk.shape[0] for chunk in sources[0])
    smem = pl.BlockSpec(memory_space=pltpu.SMEM)
    anywhere = pl.BlockSpec(memory_space=pl.ANY)
    flat = [chunk for slot in sources for chunk in slot]
    n_tiles = tiles.shape[0]
    return pl.pallas_call(
        functools.partial(history_kernel, first, count, kept, n_hist, n_row, n_chunks),
        out_shape=[
            jax.ShapeDtypeStruct((count * illum, size), jnp.float32 if d == 0 else jnp.bfloat16)
            for d in range(n_hist)
        ],
        in_specs=[smem] * 5 + [anywhere] * (len(flat) + 1),
        out_specs=[pl.BlockSpec(memory_space=pltpu.VMEM)] * n_hist,
        scratch_shapes=[
            pltpu.VMEM((len(sources), held_rows, size), jnp.bfloat16),
            pltpu.VMEM((n_tiles, size, size), jnp.bfloat16),
            pltpu.VMEM((n_hist, count * illum, size), jnp.float32),
            pltpu.SemaphoreType.DMA((len(sources), n_chunks)),
            pltpu.SemaphoreType.DMA((n_tiles // BATCH,)),
        ],
        compiler_params=pltpu.CompilerParams(vmem_limit_bytes=48 << 20),
        cost_estimate=pl.CostEstimate(
            flops=2 * n_tiles * count * illum * size * size,
            bytes_accessed=2 * n_tiles * size * size,
            transcendentals=0,
        ),
    )(pos, rows, cols, lags, scales, *flat, tiles)


def on_device(
    incident, past, hist_tiles, tile_rows, tile_cols, tile_lags, tile_scales, near_tiles, inverses
):
    n_hist, n_row = lax.axis_size("hist"), lax.axis_size("row")
    core = lax.axis_index("cur")
    steps, _, size, illum = incident.shape
    kept = past.shape[1]
    spans = near_tiles.shape[1]
    offsets = near_tiles.shape[2]
    chips = ("hist", "row")
    pos = jnp.stack([lax.axis_index("hist"), lax.axis_index("row"), core]).astype(jnp.int32)
    incident = jnp.swapaxes(incident[:, 0], 1, 2)
    past = jnp.swapaxes(past[0], 1, 2)
    early = past[: kept - 3].reshape((kept - 3) * illum, size)
    late = past[kept - 3 :].reshape(3 * illum, size)

    along = [[early, late]]
    for distance in range(1, n_row):
        along.append([rotated(early, "row", distance)])
    for distance in range(1, n_row):
        along[distance].append(rotated(late, "row", distance))
    across = [[swapped(chunk) for chunk in slot] for slot in along]
    sources = along + across

    tables = (tile_rows[0], tile_cols[0], tile_lags[0], tile_scales[0])

    def reduced(parts):
        total = parts[0]
        for distance in range(1, n_hist):
            route = [(i, partner(i, distance, n_hist)) for i in range(n_hist)]
            total = total + lax.ppermute(parts[distance], "hist", route).astype(jnp.float32)
        return halved(total.reshape(-1, illum, size))

    parts = history_parts(
        [slot[:1] for slot in sources], hist_tiles[0], *tables, pos, 0, 1, kept, illum, n_hist, n_row
    )
    first_history = reduced(parts)
    parts = history_parts(
        sources, hist_tiles[0], *tables, pos, 1, steps - 1, kept, illum, n_hist, n_row
    )
    later_history = reduced(parts)

    near = in_order(near_tiles[0], swapped(near_tiles[0]))
    inverse = in_order(inverses[0], swapped(inverses[0]))
    own = halved(jnp.concatenate([incident, past[kept - 3 :]], axis=0))
    incident, window = own[:, :steps].astype(jnp.float32), own[:, steps:]

    def neighbours(block):
        return jnp.concatenate([shifted(block, chips, 1), block, shifted(block, chips, -1)], axis=0)

    def coupled(sources, lag):
        return jnp.stack(
            [
                jnp.einsum(
                    "orj,oij->ri",
                    sources[q : q + offsets],
                    near[q, lag - 1],
                    preferred_element_type=jnp.float32,
                )
                for q in range(2)
            ]
        )

    around = neighbours(window)
    held = {step - 3: around[:, step] for step in range(3)}
    made = []
    for step in range(steps):
        history = first_history[:, 0] if step == 0 else later_history[:, step - 1]
        ready = incident[:, step] - history
        for lag in range(spans, 0, -1):
            ready = ready - coupled(held[step - lag], lag)
        rhs = ready.astype(jnp.bfloat16)
        fresh = jnp.einsum(
            "qrj,qij->qri", rhs, inverse, preferred_element_type=jnp.float32
        ).astype(jnp.bfloat16)
        made.append(fresh)
        if step + 1 < steps:
            held[step] = neighbours(fresh)

    made = jnp.stack(made, axis=1)
    lower = core == 0
    mine = jnp.where(lower, made[0], made[1])
    other = swapped(jnp.where(lower, made[1], made[0]))
    whole = jnp.concatenate(
        [jnp.where(lower, mine, other), jnp.where(lower, other, mine)], axis=1
    )
    return jnp.swapaxes(whole, 1, 2)[:, None]


def solution(mesh):
    every = ("hist", "row", "cur")
    placed = (
        P(None, every, None, None),
        P(every, None, None, None),
        P(every, None, None, None),
        P(every, None),
        P(every, None),
        P(every, None),
        P(every, None),
        P(every, None, None, None, None),
        P(every, None, None),
    )
    return jax.shard_map(
        on_device,
        mesh=mesh,
        in_specs=placed,
        out_specs=P(None, every, None, None),
        check_vma=False,
    )
```

```python
import functools

import jax
import jax.numpy as jnp
from jax import lax
from jax.experimental import pallas as pl
from jax.experimental.pallas import tpu as pltpu
from jax.sharding import PartitionSpec as P


BATCH = 8


def partner(me, distance, count):
    if count & (count - 1) == 0:
        return me ^ distance
    return (me + distance) % count


def permuted(block, axis, route):
    return lax.ppermute(block, axis, route)


def swapped(block):
    return lax.ppermute(block, "cur", [(0, 1), (1, 0)])


def in_order(mine, theirs):
    lower = lax.axis_index("cur") == 0
    return jnp.stack([jnp.where(lower, mine, theirs), jnp.where(lower, theirs, mine)])


def halves(block):
    half = block.shape[-2] // 2
    return lax.dynamic_slice_in_dim(block, lax.axis_index("cur") * half, half, block.ndim - 2)


def halved(block):
    half = block.shape[-2] // 2
    others = lax.dynamic_slice_in_dim(
        block, (1 - lax.axis_index("cur")) * half, half, block.ndim - 2
    )
    return in_order(halves(block), swapped(others))


def place_of(column, row, core):
    return lax.bitwise_xor(lax.div(column, 2), row), jnp.where(lax.rem(column, 2) == core, 0, 1)


def partner_index(row, me, count):
    if count & (count - 1) == 0:
        return lax.bitwise_xor(row, me)
    return lax.rem(row - me + count, count)


def accumulate(number, first, illum, kept, steps, n_hist, tables, tiles, held, total):
    pos, rows, cols, lags, scales, lists, counts = tables
    count = counts[number]

    def body(batch, carry):
        for inner in range(BATCH):
            at = batch * BATCH + inner
            real = at < count
            tile = lists[number, jnp.where(real, at, 0)]
            scale = jnp.where(real, scales[tile], 0.0)
            target = partner_index(rows[tile], pos[0], n_hist)
            place, which = place_of(cols[tile], pos[1], pos[2])
            start = pl.multiple_of((kept - lags[tile]) * illum, illum)
            x = held[(place - first) * 2 + which, pl.ds(start, steps * illum), :]
            y = lax.dot_general(
                x, tiles[tile], (((1,), (1,)), ((), ())), preferred_element_type=jnp.float32
            )
            total[target] += y * scale
        return carry

    lax.fori_loop(0, lax.div(count + BATCH - 1, BATCH), body, 0)


def opening_kernel(illum, kept, steps, n_hist, *refs):
    pos, rows, cols, lags, scales, tiles, held, total, lists, counts = refs
    total[...] = jnp.zeros_like(total)

    def choose(tile, so_far):
        place, _ = place_of(cols[tile], pos[1], pos[2])
        nexts = []
        for number in range(2):
            lists[number, so_far[number]] = tile
            mine = place == 3 if number == 1 else place != 3
            nexts.append(so_far[number] + jnp.where(mine, 1, 0))
        return tuple(nexts)

    for number, count in enumerate(lax.fori_loop(0, tiles.shape[0], choose, (0, 0), unroll=4)):
        counts[number] = count
    tables = (pos, rows, cols, lags, scales, lists, counts)
    accumulate(0, 0, illum, kept, steps, n_hist, tables, tiles, held, total)


def stage_kernel(number, first, illum, kept, steps, n_hist, closing, *refs):
    tables, tiles, held = refs[:7], refs[7], refs[8]
    total, *outs = refs[10:]
    accumulate(number, first, illum, kept, steps, n_hist, tables, tiles, held, total)
    if closing:
        for distance in range(1, n_hist):
            outs[distance - 1][...] = total[distance].astype(jnp.bfloat16)


def estimate(tiles, rows):
    n_tiles, size = tiles.shape[0], tiles.shape[-1]
    return pl.CostEstimate(
        flops=n_tiles * rows * size * size, bytes_accessed=n_tiles * size * size, transcendentals=0
    )


def opening(tables, tiles, held, illum, kept, steps, n_hist):
    smem, vmem = pl.BlockSpec(memory_space=pltpu.SMEM), pl.BlockSpec(memory_space=pltpu.VMEM)
    n_tiles, size = tiles.shape[0], tiles.shape[-1]
    return pl.pallas_call(
        functools.partial(opening_kernel, illum, kept, steps, n_hist),
        out_shape=[
            jax.ShapeDtypeStruct((n_hist, steps * illum, size), jnp.float32),
            jax.ShapeDtypeStruct((2, n_tiles + BATCH), jnp.int32),
            jax.ShapeDtypeStruct((2,), jnp.int32),
        ],
        in_specs=[smem] * 5 + [vmem] * 2,
        out_specs=[vmem, smem, smem],
        compiler_params=pltpu.CompilerParams(vmem_limit_bytes=8 << 20),
        cost_estimate=estimate(tiles, steps * illum),
        name="opening",
    )(*tables, tiles, held)


def stage(number, tables, tiles, first, held, total, illum, kept, steps, n_hist, closing):
    smem, vmem = pl.BlockSpec(memory_space=pltpu.SMEM), pl.BlockSpec(memory_space=pltpu.VMEM)
    size = tiles.shape[-1]
    out_shape = [jax.ShapeDtypeStruct(total.shape, total.dtype)]
    if closing:
        out_shape += [jax.ShapeDtypeStruct((steps * illum, size), jnp.bfloat16)] * (n_hist - 1)
    return pl.pallas_call(
        functools.partial(stage_kernel, number, first, illum, kept, steps, n_hist, closing),
        out_shape=out_shape,
        in_specs=[smem] * 7 + [vmem] * 3,
        out_specs=[vmem] * len(out_shape),
        input_output_aliases={9: 0},
        compiler_params=pltpu.CompilerParams(vmem_limit_bytes=8 << 20),
        cost_estimate=estimate(tiles, steps * illum),
    )(*tables, tiles, held, total)


def on_device(
    incident, past, hist_tiles, tile_rows, tile_cols, tile_lags, tile_scales, near_tiles, inverses
):
    n_hist, n_row = lax.axis_size("hist"), lax.axis_size("row")
    core = lax.axis_index("cur")
    row = lax.axis_index("row")
    steps, _, size, illum = incident.shape
    kept = past.shape[1]
    spans = near_tiles.shape[1]
    offsets = near_tiles.shape[2]
    half = illum // 2
    chips = ("hist", "row")
    n_chips = n_hist * n_row
    pos = jnp.stack([lax.axis_index("hist"), row, core]).astype(jnp.int32)
    incident = jnp.swapaxes(incident[:, 0], 1, 2)
    past = jnp.swapaxes(past[0], 1, 2)
    stored = past.reshape(kept * illum, size)

    two_away = permuted(stored, "row", [(i, i ^ 2) for i in range(n_row)])
    beside = permuted(stored, "row", [(i, i ^ 1) for i in range(n_row)])

    own = jnp.stack([stored, swapped(stored)])
    incident = in_order(halves(incident), halves(swapped(incident))).astype(jnp.float32)
    near = in_order(near_tiles[0], swapped(near_tiles[0]))
    inverse = in_order(inverses[0], swapped(inverses[0]))

    def recent(pair):
        last = halves(pair.reshape(2, kept, illum, size)[:, kept - spans :])
        return in_order(last[0], last[1])

    upper = [(i, i + 1) for i in range(1, n_chips - 1, 2)]
    upper = upper + [(n_chips - 1, 0)]
    upper = upper + [(j, i) for i, j in upper]
    lower = [(i, i + 1) for i in range(0, n_chips - 1, 2)]
    lower = lower + [(j, i) for i, j in lower]
    odd = row % 2 == 1
    chip = lax.axis_index("hist") * n_row + row
    at_end = (chip == 0) | (chip == n_chips - 1)

    def neighbours(block):
        first = permuted(block, chips, upper)
        second = permuted(block, chips, lower)
        return first, block, second

    def arranged(first, block, second):
        first = jnp.where(at_end, jnp.zeros_like(first), first)
        before = jnp.where(odd, second, first)
        after = jnp.where(odd, first, second)
        return jnp.concatenate([before, block, after], axis=0)

    def coupled(sources, lag):
        return jnp.stack(
            [
                jnp.einsum(
                    "orj,oij->ri",
                    sources[q : q + offsets],
                    near[q, lag - 1],
                    preferred_element_type=jnp.float32,
                )
                for q in range(2)
            ]
        )

    tables = (pos, tile_rows[0], tile_cols[0], tile_lags[0], tile_scales[0])
    sizes = (illum, kept, steps, n_hist)

    window = recent(own)
    across = permuted(past[kept - spans :], chips, upper)
    far = permuted(two_away, "row", [(i, i ^ 1) for i in range(n_row)])
    held = jnp.stack([part for block in (beside, two_away) for part in (block, swapped(block))])
    held = jnp.concatenate([own, held], axis=0)
    total, *lists = opening(tables, hist_tiles[0], held, *sizes)
    tables = (*tables, *lists)
    far, total = lax.optimization_barrier((far, total))
    pair = jnp.stack([far, swapped(far)])
    total, *parts = stage(1, tables, hist_tiles[0], 3, pair, total, *sizes, True)

    order = sorted(range(1, n_hist), key=lambda d: -bin(d).count("1"))
    arrived = []
    for distance in order:
        route = [(i, partner(i, distance, n_hist)) for i in range(n_hist)]
        arrived.append(permuted(parts[distance - 1], "hist", route))

    across, held, total = lax.optimization_barrier((across, held, total))
    around = arranged(halved(across), window, recent(held[2:4]))
    base = [incident[:, step] for step in range(steps)]
    for lag in range(1, spans + 1):
        terms = coupled(around[:, spans - lag :].reshape(-1, lag * half, size), lag)
        terms = terms.reshape(2, lag, half, size)
        for step in range(min(lag, steps)):
            base[step] = base[step] - terms[:, step]
    total = total[0]
    for block in arrived:
        total = total + block.astype(jnp.float32)
    history = halved(total.reshape(steps, illum, size))

    made = []
    for step in range(steps):
        ready = base[step] - history[:, step]
        if step > 0:
            ready = ready - coupled(latest, 1)
        rhs = ready.astype(jnp.bfloat16)
        fresh = jnp.einsum(
            "qrj,qij->qri", rhs, inverse, preferred_element_type=jnp.float32
        ).astype(jnp.bfloat16)
        made.append(fresh)
        if step + 1 < steps:
            arriving = neighbours(fresh)
            if step > 0:
                latest, _ = lax.optimization_barrier((latest, fresh))
                for lag in range(2, spans + 1):
                    if step - 1 + lag < steps:
                        base[step - 1 + lag] = base[step - 1 + lag] - coupled(latest, lag)
            latest = arranged(*arriving)

    first = core == 0

    def rejoined(block):
        mine = jnp.where(first, block[0], block[1])
        other = swapped(jnp.where(first, block[1], block[0]))
        return jnp.concatenate(
            [jnp.where(first, mine, other), jnp.where(first, other, mine)], axis=-2
        )

    whole = rejoined(jnp.stack(made[:-1], axis=1))
    whole = jnp.concatenate([whole, rejoined(made[-1])[None]], axis=0)
    return jnp.swapaxes(whole, 1, 2)[:, None]


def solution(mesh):
    every = ("hist", "row", "cur")
    placed = (
        P(None, every, None, None),
        P(every, None, None, None),
        P(every, None, None, None),
        P(every, None),
        P(every, None),
        P(every, None),
        P(every, None),
        P(every, None, None, None, None),
        P(every, None, None),
    )

    return jax.shard_map(
        on_device,
        mesh=mesh,
        in_specs=placed,
        out_specs=P(None, every, None, None),
        check_vma=False,
    )
```

```python
import functools

import jax
import jax.numpy as jnp
from jax import lax
from jax.experimental import pallas as pl
from jax.experimental.pallas import tpu as pltpu
from jax.sharding import PartitionSpec as P


BATCH = 8


def partner(me, distance, count):
    if count & (count - 1) == 0:
        return me ^ distance
    return (me + distance) % count


def permuted(block, axis, route):
    return lax.ppermute(block, axis, route)


def swapped(block):
    return lax.ppermute(block, "cur", [(0, 1), (1, 0)])


def in_order(mine, theirs):
    lower = lax.axis_index("cur") == 0
    return jnp.stack([jnp.where(lower, mine, theirs), jnp.where(lower, theirs, mine)])


def halves(block):
    half = block.shape[-2] // 2
    return lax.dynamic_slice_in_dim(block, lax.axis_index("cur") * half, half, block.ndim - 2)


def halved(block):
    half = block.shape[-2] // 2
    others = lax.dynamic_slice_in_dim(
        block, (1 - lax.axis_index("cur")) * half, half, block.ndim - 2
    )
    return in_order(halves(block), swapped(others))


def place_of(column, row, core):
    return lax.bitwise_xor(lax.div(column, 2), row), jnp.where(lax.rem(column, 2) == core, 0, 1)


def partner_index(row, me, count):
    if count & (count - 1) == 0:
        return lax.bitwise_xor(row, me)
    return lax.rem(row - me + count, count)


def accumulate(number, first, illum, kept, steps, n_hist, tables, tiles, held, total):
    pos, rows, cols, lags, scales, lists, counts = tables
    count = counts[number]

    def body(batch, carry):
        for inner in range(BATCH):
            at = batch * BATCH + inner
            real = at < count
            tile = lists[number, jnp.where(real, at, 0)]
            scale = jnp.where(real, scales[tile], 0.0)
            target = partner_index(rows[tile], pos[0], n_hist)
            place, which = place_of(cols[tile], pos[1], pos[2])
            start = pl.multiple_of((kept - lags[tile]) * illum, illum)
            x = held[(place - first) * 2 + which, pl.ds(start, steps * illum), :]
            y = lax.dot_general(
                x, tiles[tile], (((1,), (1,)), ((), ())), preferred_element_type=jnp.float32
            )
            total[target] += y * scale
        return carry

    lax.fori_loop(0, lax.div(count + BATCH - 1, BATCH), body, 0)


def listing_kernel(*refs):
    pos, cols, _, lists, counts = refs

    def choose(tile, so_far):
        place, _ = place_of(cols[tile], pos[1], pos[2])
        nexts = []
        for number in range(2):
            lists[number, so_far[number]] = tile
            mine = place == 3 if number == 1 else place != 3
            nexts.append(so_far[number] + jnp.where(mine, 1, 0))
        return tuple(nexts)

    for number, count in enumerate(lax.fori_loop(0, cols.shape[0], choose, (0, 0), unroll=4)):
        counts[number] = count


def opening_kernel(illum, kept, steps, n_hist, *refs):
    tables, tiles, held, total = refs[:7], refs[7], refs[8], refs[9]
    total[...] = jnp.zeros_like(total)
    accumulate(0, 0, illum, kept, steps, n_hist, tables, tiles, held, total)


def stage_kernel(number, first, illum, kept, steps, n_hist, closing, *refs):
    tables, tiles, held = refs[:7], refs[7], refs[8]
    total, *outs = refs[10:]
    accumulate(number, first, illum, kept, steps, n_hist, tables, tiles, held, total)
    if closing:
        for distance in range(1, n_hist):
            outs[distance - 1][...] = total[distance].astype(jnp.bfloat16)


def estimate(tiles, rows):
    n_tiles, size = tiles.shape[0], tiles.shape[-1]
    return pl.CostEstimate(
        flops=n_tiles * rows * size * size, bytes_accessed=n_tiles * size * size, transcendentals=0
    )


def listing(pos, cols, tiles):
    smem, vmem = pl.BlockSpec(memory_space=pltpu.SMEM), pl.BlockSpec(memory_space=pltpu.VMEM)
    return pl.pallas_call(
        listing_kernel,
        out_shape=[
            jax.ShapeDtypeStruct((2, cols.shape[0] + BATCH), jnp.int32),
            jax.ShapeDtypeStruct((2,), jnp.int32),
        ],
        in_specs=[smem] * 2 + [vmem],
        out_specs=[smem, smem],
        compiler_params=pltpu.CompilerParams(vmem_limit_bytes=8 << 20),
        name="listing",
    )(pos, cols, tiles)


def opening(tables, tiles, held, illum, kept, steps, n_hist):
    smem, vmem = pl.BlockSpec(memory_space=pltpu.SMEM), pl.BlockSpec(memory_space=pltpu.VMEM)
    size = tiles.shape[-1]
    return pl.pallas_call(
        functools.partial(opening_kernel, illum, kept, steps, n_hist),
        out_shape=jax.ShapeDtypeStruct((n_hist, steps * illum, size), jnp.float32),
        in_specs=[smem] * 7 + [vmem] * 2,
        out_specs=vmem,
        compiler_params=pltpu.CompilerParams(vmem_limit_bytes=8 << 20),
        cost_estimate=estimate(tiles, steps * illum),
        name="opening",
    )(*tables, tiles, held)


def stage(number, tables, tiles, first, held, total, illum, kept, steps, n_hist, closing):
    smem, vmem = pl.BlockSpec(memory_space=pltpu.SMEM), pl.BlockSpec(memory_space=pltpu.VMEM)
    size = tiles.shape[-1]
    out_shape = [jax.ShapeDtypeStruct(total.shape, total.dtype)]
    if closing:
        out_shape += [jax.ShapeDtypeStruct((steps * illum, size), jnp.bfloat16)] * (n_hist - 1)
    return pl.pallas_call(
        functools.partial(stage_kernel, number, first, illum, kept, steps, n_hist, closing),
        out_shape=out_shape,
        in_specs=[smem] * 7 + [vmem] * 3,
        out_specs=[vmem] * len(out_shape),
        input_output_aliases={9: 0},
        compiler_params=pltpu.CompilerParams(vmem_limit_bytes=8 << 20),
        cost_estimate=estimate(tiles, steps * illum),
    )(*tables, tiles, held, total)


def on_device(
    incident, past, hist_tiles, tile_rows, tile_cols, tile_lags, tile_scales, near_tiles, inverses
):
    n_hist, n_row = lax.axis_size("hist"), lax.axis_size("row")
    core = lax.axis_index("cur")
    row = lax.axis_index("row")
    steps, _, size, illum = incident.shape
    kept = past.shape[1]
    spans = near_tiles.shape[1]
    offsets = near_tiles.shape[2]
    half = illum // 2
    chips = ("hist", "row")
    n_chips = n_hist * n_row
    pos = jnp.stack([lax.axis_index("hist"), row, core]).astype(jnp.int32)
    incident = jnp.swapaxes(incident[:, 0], 1, 2)
    past = jnp.swapaxes(past[0], 1, 2)
    stored = past.reshape(kept * illum, size)

    two_away = permuted(stored, "row", [(i, i ^ 2) for i in range(n_row)])
    beside = permuted(stored, "row", [(i, i ^ 1) for i in range(n_row)])

    own = jnp.stack([stored, swapped(stored)])
    incident = in_order(halves(incident), halves(swapped(incident))).astype(jnp.float32)
    near = in_order(near_tiles[0], swapped(near_tiles[0]))
    inverse = in_order(inverses[0], swapped(inverses[0]))

    def recent(pair):
        last = halves(pair.reshape(2, kept, illum, size)[:, kept - spans :])
        return in_order(last[0], last[1])

    upper = [(i, i + 1) for i in range(1, n_chips - 1, 2)]
    upper = upper + [(n_chips - 1, 0)]
    upper = upper + [(j, i) for i, j in upper]
    lower = [(i, i + 1) for i in range(0, n_chips - 1, 2)]
    lower = lower + [(j, i) for i, j in lower]
    odd = row % 2 == 1
    chip = lax.axis_index("hist") * n_row + row
    at_end = (chip == 0) | (chip == n_chips - 1)

    def neighbours(block):
        first = permuted(block, chips, upper)
        second = permuted(block, chips, lower)
        return first, block, second

    def arranged(first, block, second):
        first = jnp.where(at_end, jnp.zeros_like(first), first)
        before = jnp.where(odd, second, first)
        after = jnp.where(odd, first, second)
        return jnp.concatenate([before, block, after], axis=0)

    def coupled(sources, lag):
        return jnp.stack(
            [
                jnp.einsum(
                    "orj,oij->ri",
                    sources[q : q + offsets],
                    near[q, lag - 1],
                    preferred_element_type=jnp.float32,
                )
                for q in range(2)
            ]
        )

    tables = (pos, tile_rows[0], tile_cols[0], tile_lags[0], tile_scales[0])
    sizes = (illum, kept, steps, n_hist)

    window = recent(own)
    across = permuted(past[kept - spans :], chips, upper)
    lists = listing(pos, tile_cols[0], hist_tiles[0])
    two_away, *lists = lax.optimization_barrier((two_away, *lists))
    tables = (*tables, *lists)
    far = permuted(two_away, "row", [(i, i ^ 1) for i in range(n_row)])
    held = jnp.stack([part for block in (beside, two_away) for part in (block, swapped(block))])
    held = jnp.concatenate([own, held], axis=0)
    total = opening(tables, hist_tiles[0], held, *sizes)
    far, total = lax.optimization_barrier((far, total))
    pair = jnp.stack([far, swapped(far)])
    total, *parts = stage(1, tables, hist_tiles[0], 3, pair, total, *sizes, True)

    order = sorted(range(1, n_hist), key=lambda d: -bin(d).count("1"))
    arrived = []
    for distance in order:
        route = [(i, partner(i, distance, n_hist)) for i in range(n_hist)]
        arrived.append(permuted(parts[distance - 1], "hist", route))

    across, held, total = lax.optimization_barrier((across, held, total))
    around = arranged(halved(across), window, recent(held[2:4]))
    base = [incident[:, step] for step in range(steps)]
    for lag in range(1, spans + 1):
        terms = coupled(around[:, spans - lag :].reshape(-1, lag * half, size), lag)
        terms = terms.reshape(2, lag, half, size)
        for step in range(min(lag, steps)):
            base[step] = base[step] - terms[:, step]
    total = total[0]
    for block in arrived:
        total = total + block.astype(jnp.float32)
    history = halved(total.reshape(steps, illum, size))

    made = []
    for step in range(steps):
        ready = base[step] - history[:, step]
        if step > 0:
            ready = ready - coupled(latest, 1)
        rhs = ready.astype(jnp.bfloat16)
        fresh = jnp.einsum(
            "qrj,qij->qri", rhs, inverse, preferred_element_type=jnp.float32
        ).astype(jnp.bfloat16)
        made.append(fresh)
        if step + 1 < steps:
            arriving = neighbours(fresh)
            if step > 0:
                latest, _ = lax.optimization_barrier((latest, fresh))
                for lag in range(2, spans + 1):
                    if step - 1 + lag < steps:
                        base[step - 1 + lag] = base[step - 1 + lag] - coupled(latest, lag)
            latest = arranged(*arriving)

    first = core == 0

    def rejoined(block):
        mine = jnp.where(first, block[0], block[1])
        other = swapped(jnp.where(first, block[1], block[0]))
        return jnp.concatenate(
            [jnp.where(first, mine, other), jnp.where(first, other, mine)], axis=-2
        )

    whole = rejoined(jnp.stack(made[:-1], axis=1))
    whole = jnp.concatenate([whole, rejoined(made[-1])[None]], axis=0)
    return jnp.swapaxes(whole, 1, 2)[:, None]


def solution(mesh):
    every = ("hist", "row", "cur")
    placed = (
        P(None, every, None, None),
        P(every, None, None, None),
        P(every, None, None, None),
        P(every, None),
        P(every, None),
        P(every, None),
        P(every, None),
        P(every, None, None, None, None),
        P(every, None, None),
    )

    return jax.shard_map(
        on_device,
        mesh=mesh,
        in_specs=placed,
        out_specs=P(None, every, None, None),
        check_vma=False,
    )
```

```python
import functools

import jax
import jax.numpy as jnp
from jax import lax
from jax.experimental import pallas as pl
from jax.experimental.pallas import tpu as pltpu
from jax.sharding import PartitionSpec as P


BATCH = 16


def partner(me, distance, count):
    if count & (count - 1) == 0:
        return me ^ distance
    return (me + distance) % count


def permuted(block, axis, route):
    return lax.ppermute(block, axis, route)


def swapped(block):
    return lax.ppermute(block, "cur", [(0, 1), (1, 0)])


def in_order(mine, theirs):
    lower = lax.axis_index("cur") == 0
    return jnp.stack([jnp.where(lower, mine, theirs), jnp.where(lower, theirs, mine)])


def halves(block):
    half = block.shape[-2] // 2
    return lax.dynamic_slice_in_dim(block, lax.axis_index("cur") * half, half, block.ndim - 2)


def halved(block):
    half = block.shape[-2] // 2
    others = lax.dynamic_slice_in_dim(
        block, (1 - lax.axis_index("cur")) * half, half, block.ndim - 2
    )
    return in_order(halves(block), swapped(others))


def place_of(column, row, core):
    return lax.bitwise_xor(lax.div(column, 2), row), jnp.where(lax.rem(column, 2) == core, 0, 1)


def partner_index(row, me, count):
    if count & (count - 1) == 0:
        return lax.bitwise_xor(row, me)
    return lax.rem(row - me + count, count)


def accumulate(listed, first, illum, kept, steps, n_hist, tables, tiles, held, total):
    pos, rows, cols, lags, scales, lists, counts = tables
    count = counts[listed]

    def several(begin, number, masked):
        for inner in range(number):
            at = begin + inner
            real = at < count
            tile = lists[listed, jnp.where(real, at, 0) if masked else at]
            scale = jnp.where(real, scales[tile], 0.0) if masked else scales[tile]
            target = partner_index(rows[tile], pos[0], n_hist)
            place, which = place_of(cols[tile], pos[1], pos[2])
            start = pl.multiple_of((kept - lags[tile]) * illum, illum)
            x = held[(place - first) * 2 + which, pl.ds(start, steps * illum), :]
            y = lax.dot_general(
                x, tiles[tile], (((1,), (1,)), ((), ())), preferred_element_type=jnp.float32
            )
            total[target] += y * scale

    def body(batch, carry):
        several(batch * BATCH, BATCH, False)
        return carry

    whole = lax.div(count, BATCH)
    rest = lax.rem(count, BATCH)
    lax.fori_loop(0, whole, body, 0)

    @pl.when(rest > BATCH // 2)
    def _():
        several(whole * BATCH, BATCH, True)

    @pl.when((rest > 0) & (rest <= BATCH // 2))
    def _():
        several(whole * BATCH, BATCH // 2, True)


def listing_kernel(*refs):
    pos, cols, _, lists, counts = refs

    def choose(tile, so_far):
        place, _ = place_of(cols[tile], pos[1], pos[2])
        nexts = []
        for number in range(2):
            lists[number, so_far[number]] = tile
            mine = place == 3 if number == 1 else place != 3
            nexts.append(so_far[number] + jnp.where(mine, 1, 0))
        return tuple(nexts)

    for number, count in enumerate(lax.fori_loop(0, cols.shape[0], choose, (0, 0), unroll=4)):
        counts[number] = count


def opening_kernel(illum, kept, steps, n_hist, *refs):
    tables, tiles, held, total = refs[:7], refs[7], refs[8], refs[9]
    total[...] = jnp.zeros_like(total)
    accumulate(0, 0, illum, kept, steps, n_hist, tables, tiles, held, total)


def stage_kernel(number, first, illum, kept, steps, n_hist, closing, *refs):
    tables, tiles, held = refs[:7], refs[7], refs[8]
    total, *outs = refs[10:]
    accumulate(number, first, illum, kept, steps, n_hist, tables, tiles, held, total)
    if closing:
        for distance in range(1, n_hist):
            outs[distance - 1][...] = total[distance].astype(jnp.bfloat16)


def estimate(tiles, rows):
    n_tiles, size = tiles.shape[0], tiles.shape[-1]
    return pl.CostEstimate(
        flops=n_tiles * rows * size * size, bytes_accessed=n_tiles * size * size, transcendentals=0
    )


def listing(pos, cols, tiles):
    smem, vmem = pl.BlockSpec(memory_space=pltpu.SMEM), pl.BlockSpec(memory_space=pltpu.VMEM)
    return pl.pallas_call(
        listing_kernel,
        out_shape=[
            jax.ShapeDtypeStruct((2, cols.shape[0] + BATCH), jnp.int32),
            jax.ShapeDtypeStruct((2,), jnp.int32),
        ],
        in_specs=[smem] * 2 + [vmem],
        out_specs=[smem, smem],
        compiler_params=pltpu.CompilerParams(vmem_limit_bytes=8 << 20),
        name="listing",
    )(pos, cols, tiles)


def opening(tables, tiles, held, illum, kept, steps, n_hist):
    smem, vmem = pl.BlockSpec(memory_space=pltpu.SMEM), pl.BlockSpec(memory_space=pltpu.VMEM)
    size = tiles.shape[-1]
    return pl.pallas_call(
        functools.partial(opening_kernel, illum, kept, steps, n_hist),
        out_shape=jax.ShapeDtypeStruct((n_hist, steps * illum, size), jnp.float32),
        in_specs=[smem] * 7 + [vmem] * 2,
        out_specs=vmem,
        compiler_params=pltpu.CompilerParams(vmem_limit_bytes=8 << 20),
        cost_estimate=estimate(tiles, steps * illum),
        name="opening",
    )(*tables, tiles, held)


def stage(number, tables, tiles, first, held, total, illum, kept, steps, n_hist, closing):
    smem, vmem = pl.BlockSpec(memory_space=pltpu.SMEM), pl.BlockSpec(memory_space=pltpu.VMEM)
    size = tiles.shape[-1]
    out_shape = [jax.ShapeDtypeStruct(total.shape, total.dtype)]
    if closing:
        out_shape += [jax.ShapeDtypeStruct((steps * illum, size), jnp.bfloat16)] * (n_hist - 1)
    return pl.pallas_call(
        functools.partial(stage_kernel, number, first, illum, kept, steps, n_hist, closing),
        out_shape=out_shape,
        in_specs=[smem] * 7 + [vmem] * 3,
        out_specs=[vmem] * len(out_shape),
        input_output_aliases={9: 0},
        compiler_params=pltpu.CompilerParams(vmem_limit_bytes=8 << 20),
        cost_estimate=estimate(tiles, steps * illum),
    )(*tables, tiles, held, total)


def on_device(
    incident, past, hist_tiles, tile_rows, tile_cols, tile_lags, tile_scales, near_tiles, inverses
):
    n_hist, n_row = lax.axis_size("hist"), lax.axis_size("row")
    core = lax.axis_index("cur")
    row = lax.axis_index("row")
    steps, _, size, illum = incident.shape
    kept = past.shape[1]
    spans = near_tiles.shape[1]
    offsets = near_tiles.shape[2]
    half = illum // 2
    chips = ("hist", "row")
    n_chips = n_hist * n_row
    pos = jnp.stack([lax.axis_index("hist"), row, core]).astype(jnp.int32)
    incident = jnp.swapaxes(incident[:, 0], 1, 2)
    past = jnp.swapaxes(past[0], 1, 2)
    stored = past.reshape(kept * illum, size)

    two_away = permuted(stored, "row", [(i, i ^ 2) for i in range(n_row)])
    beside = permuted(stored, "row", [(i, i ^ 1) for i in range(n_row)])

    own = jnp.stack([stored, swapped(stored)])
    incident = in_order(halves(incident), halves(swapped(incident))).astype(jnp.float32)
    near = in_order(near_tiles[0], swapped(near_tiles[0]))
    inverse = in_order(inverses[0], swapped(inverses[0]))

    def recent(pair):
        last = halves(pair.reshape(2, kept, illum, size)[:, kept - spans :])
        return in_order(last[0], last[1])

    upper = [(i, i + 1) for i in range(1, n_chips - 1, 2)]
    upper = upper + [(n_chips - 1, 0)]
    upper = upper + [(j, i) for i, j in upper]
    lower = [(i, i + 1) for i in range(0, n_chips - 1, 2)]
    lower = lower + [(j, i) for i, j in lower]
    odd = row % 2 == 1
    chip = lax.axis_index("hist") * n_row + row
    at_end = (chip == 0) | (chip == n_chips - 1)

    def neighbours(block):
        first = permuted(block, chips, upper)
        second = permuted(block, chips, lower)
        return first, block, second

    def arranged(first, block, second):
        first = jnp.where(at_end, jnp.zeros_like(first), first)
        before = jnp.where(odd, second, first)
        after = jnp.where(odd, first, second)
        return jnp.concatenate([before, block, after], axis=0)

    def coupled(sources, lag):
        return jnp.stack(
            [
                jnp.einsum(
                    "orj,oij->ri",
                    sources[q : q + offsets],
                    near[q, lag - 1],
                    preferred_element_type=jnp.float32,
                )
                for q in range(2)
            ]
        )

    tables = (pos, tile_rows[0], tile_cols[0], tile_lags[0], tile_scales[0])
    sizes = (illum, kept, steps, n_hist)

    window = recent(own)
    ends = [(i, j) for i, j in upper if i // n_row != j // n_row]
    inside = [g * n_row + i for g in range(n_hist) for i in range(1, n_row - 1)]
    ends = ends + [(i, partner(i // n_row, 1, n_hist) * n_row + i % n_row) for i in inside]
    across = permuted(past[kept - spans :], chips, ends)
    lists = listing(pos, tile_cols[0], hist_tiles[0])
    two_away, *lists = lax.optimization_barrier((two_away, *lists))
    tables = (*tables, *lists)
    far = permuted(two_away, "row", [(i, i ^ 1) for i in range(n_row)])
    held = jnp.stack([part for block in (beside, two_away) for part in (block, swapped(block))])
    held = jnp.concatenate([own, held], axis=0)
    total = opening(tables, hist_tiles[0], held, *sizes)
    far, total = lax.optimization_barrier((far, total))
    pair = jnp.stack([far, swapped(far)])
    total, *parts = stage(1, tables, hist_tiles[0], 3, pair, total, *sizes, True)

    order = sorted(range(1, n_hist), key=lambda d: bin(d).count("1"))
    arrived = []
    for distance in order:
        route = [(i, partner(i, distance, n_hist)) for i in range(n_hist)]
        arrived.append(permuted(parts[distance - 1], "hist", route))

    across, held, pair, total = lax.optimization_barrier((across, held, pair, total))
    outer = (row == 0) | (row == n_row - 1)
    across = jnp.where(outer, halved(across), recent(pair))
    around = arranged(across, window, recent(held[2:4]))
    base = [incident[:, step] for step in range(steps)]
    for lag in range(1, spans + 1):
        terms = coupled(around[:, spans - lag :].reshape(-1, lag * half, size), lag)
        terms = terms.reshape(2, lag, half, size)
        for step in range(min(lag, steps)):
            base[step] = base[step] - terms[:, step]
    total = total[0]
    for block in arrived:
        total = total + block.astype(jnp.float32)
    history = halved(total.reshape(steps, illum, size))

    def from_here(block):
        return jnp.stack(
            [
                jnp.einsum(
                    "orj,oij->ri", block, near[q, 0, 2 - q : 4 - q], preferred_element_type=jnp.float32
                )
                for q in range(2)
            ]
        )

    beyond = [jnp.concatenate([near[q, 0, : 2 - q], near[q, 0, 4 - q :]], axis=0) for q in range(2)]

    def from_beside(sources):
        return jnp.stack(
            [
                jnp.einsum(
                    "orj,oij->ri",
                    jnp.concatenate([sources[q:2], sources[4 : q + 5]], axis=0),
                    beyond[q],
                    preferred_element_type=jnp.float32,
                )
                for q in range(2)
            ]
        )

    made = []
    for step in range(steps):
        ready = base[step] - history[:, step]
        if step > 0:
            ready = ready - here - from_beside(latest)
        rhs = ready.astype(jnp.bfloat16)
        fresh = jnp.einsum(
            "qrj,qij->qri", rhs, inverse, preferred_element_type=jnp.float32
        ).astype(jnp.bfloat16)
        made.append(fresh)
        if step + 1 < steps:
            arriving = neighbours(fresh)
            here = from_here(fresh)
            if step > 0:
                latest, _ = lax.optimization_barrier((latest, fresh))
                for lag in range(2, spans + 1):
                    if step - 1 + lag < steps:
                        base[step - 1 + lag] = base[step - 1 + lag] - coupled(latest, lag)
            latest = arranged(*arriving)

    first = core == 0

    def rejoined(block):
        mine = jnp.where(first, block[0], block[1])
        other = swapped(jnp.where(first, block[1], block[0]))
        return jnp.concatenate(
            [jnp.where(first, mine, other), jnp.where(first, other, mine)], axis=-2
        )

    whole = rejoined(jnp.stack(made[:-1], axis=1))
    whole = jnp.concatenate([whole, rejoined(made[-1])[None]], axis=0)
    return jnp.swapaxes(whole, 1, 2)[:, None]


def solution(mesh):
    every = ("hist", "row", "cur")
    placed = (
        P(None, every, None, None),
        P(every, None, None, None),
        P(every, None, None, None),
        P(every, None),
        P(every, None),
        P(every, None),
        P(every, None),
        P(every, None, None, None, None),
        P(every, None, None),
    )

    return jax.shard_map(
        on_device,
        mesh=mesh,
        in_specs=placed,
        out_specs=P(None, every, None, None),
        check_vma=False,
    )
```
